32 devices in a mesh: space: 4 (over x, core), chan: 8 (over z, y).
Axes of the slice: x: 2, y: 2, z: 4, core: 2. Of those that a mesh axis runs over, the one named last changes fastest.
Arguments:
- inputs: bfloat16 [768, 64, 256], P('chan', 'space'), may hold values from -6 to 6
- initial_state: bfloat16 [384, 64, 256], P('chan', 'space'), may hold values from -6 to 6
- input_weight: bfloat16 [3, 9, 768, 384], P(None, None, 'chan'), may hold values from -0.0625 to 0.0625
- hidden_weight: bfloat16 [3, 9, 384, 384], P(None, None, 'chan'), may hold values from -0.0625 to 0.0625
- gate_bias: float32 [3, 384], replicated, may hold values from -3 to 3
Outputs:
- final_state: bfloat16 [384, 64, 256], P('chan', 'space')
The draws below stay inside these ranges and needn't reach their ends.
All inputs are finite; a program needn't handle non-finite values.
Results may differ from the reference program's by a relative error of at most 0.0039.
Values may be sent and summed in bfloat16 or wider, within the bound.
A program may use at most 128 MiB of HBM per device.

```python
import jax
import jax.numpy as jnp

CIN = 768
CH = 384
W = 256
STEPS = 2
H = 64


def block_scale(stream_key, dims, cuts, least, largest):
    def one(dim, shards_of):
        steps = jax.random.uniform(jax.random.fold_in(jax.random.fold_in(stream_key, 6), dim), (shards_of,), jnp.float32, least / len(cuts), largest / len(cuts))
        return jnp.repeat(jnp.exp(steps), dims[dim] // shards_of).reshape((-1,) + (1,) * (len(dims) - dim - 1))

    factor_of = one(*cuts[0])
    for cut in cuts[1:]:
        factor_of = factor_of * one(*cut)
    return factor_of


def noise(rng, shape, scale, bound, split=(), kind=jnp.bfloat16):
    result = jax.random.normal(rng, shape, jnp.float32) * scale
    if len(split) > 0:
        result = block_scale(rng, shape, split, -0.22, 0.18) * result
    return jnp.clip(result, min=-bound, max=bound).astype(kind)


def setup_inputs(seed: int = 0) -> dict:
    key_list = jax.random.split(jax.random.key(seed), 6)
    inputs = noise(key_list[0], (CIN, H, W), 1.0, 6.0, ((0, 8), (1, 4)))
    initial_state = noise(key_list[1], (CH, H, W), 1.0, 6.0, ((0, 8), (1, 4)))
    input_weight = noise(key_list[2], (3, 9, CIN, CH), (9 * (CIN + CH)) ** -0.5, 0.0625, ((2, 8),))
    hidden_weight = noise(key_list[3], (3, 9, CH, CH), (9 * (CIN + CH)) ** -0.5, 0.0625, ((2, 8),))
    gate_bias = noise(key_list[4], (3, CH), 0.5, 3.0, (), jnp.float32)
    return dict(inputs=inputs, initial_state=initial_state, input_weight=input_weight, hidden_weight=hidden_weight, gate_bias=gate_bias)


OFFSETS = [(-1, -1), (-1, 0), (-1, 1), (0, -1), (0, 0), (0, 1), (1, -1), (1, 0), (1, 1)]


def convolve(field, weight):
    heights = field.shape[1]
    widths = field.shape[2]
    padded = jnp.pad(field, ((0, 0), (1, 1), (1, 1))).astype(jnp.float32)
    weight_wide = weight.astype(jnp.float32)
    total = jnp.zeros((weight.shape[0], weight.shape[3], heights, widths), jnp.float32)
    for tap_index, (row_off, col_off) in enumerate(OFFSETS):
        window = padded[:, 1 + row_off:1 + row_off + heights, 1 + col_off:1 + col_off + widths]
        total = total + jnp.einsum("gio,ihw->gohw", weight_wide[:, tap_index], window)
    return total


def reference(inputs, initial_state, input_weight, hidden_weight, gate_bias):
    input_terms = convolve(inputs, input_weight)
    biases = gate_bias.astype(jnp.float32)[:, :, None, None]
    current = initial_state
    for repeat in range(STEPS):
        gate_pre = convolve(current, hidden_weight[0:2])
        update = jax.nn.sigmoid(input_terms[0] + gate_pre[0] + biases[0])
        reset = jax.nn.sigmoid(input_terms[1] + gate_pre[1] + biases[1])
        gated = (reset * current.astype(jnp.float32)).astype(jnp.bfloat16)
        cand_pre = convolve(gated, hidden_weight[2:3])
        candidate = jnp.tanh(input_terms[2] + cand_pre[0] + biases[2])
        current = ((1.0 - update) * current.astype(jnp.float32) + update * candidate).astype(jnp.bfloat16)
    return current
```

```python
import functools

import jax
import jax.numpy as jnp
from jax import lax
from jax.experimental import pallas as pl
from jax.experimental.pallas import tpu as pltpu
from jax.sharding import PartitionSpec as P

STEPS = 2
MESH = pl.DeviceIdType.MESH
CORES = 2


def ring_pos(chan, n):
    return jnp.where(lax.rem(chan, 2) == 0, chan // 2, n - 1 - chan // 2)


def ring_chan(pos, n):
    return jnp.where(pos < n // 2, 2 * pos, 2 * (n - 1 - pos) + 1)


def lines(n_space):
    s = lax.axis_index("space")
    x, core = s // CORES, lax.rem(s, CORES)
    n_x = n_space // CORES
    peers = [lax.rem(x + d, n_x) * CORES + core for d in range(1, n_x)]
    return s, peers, x * CORES + 1 - core


def barrier(targets):
    sem = pltpu.get_barrier_semaphore()
    for target in targets:
        pl.semaphore_signal(sem, inc=1, device_id=target, device_id_type=MESH)
    pl.semaphore_wait(sem, len(targets))


def remote(src, dst, send, recv, target):
    return pltpu.make_async_remote_copy(
        src_ref=src, dst_ref=dst, send_sem=send, recv_sem=recv, device_id=target, device_id_type=MESH
    )


def weight_units(k_in, k_hid):
    half = k_in // 2
    right = [(0, 0, 0, k_in), (0, 2, 0, half), (1, 0, 0, k_hid)]
    left = [(0, 1, 0, k_in), (0, 2, half, half), (1, 1, 0, k_hid)]
    if k_hid % 16 == 0:
        right.append((1, 2, 0, k_hid // 2))
        left.append((1, 2, k_hid // 2, k_hid // 2))
    else:
        right.append((1, 2, 0, k_hid))
    return right, left


def spread_kernel(
    n_space, n, x_ref, win_ref, whid_ref, xall_ref, winall_ref, whidall_ref,
    a2a_send, a2a_recv, x_send, x_recv, sib_send, sib_recv, ring_send, ring_recv, local_sem,
):
    s, xpeers, sib = lines(n_space)
    me = lax.axis_index("chan")
    pos = ring_pos(me, n)
    others = [(d, ring_chan(lax.rem(pos + d, n), n)) for d in range(1, n)]
    right, left = others[0][1], others[n - 2][1]
    barrier([(s, c) for _, c in others] + [(t, me) for t in xpeers] + [(sib, me)])

    c_all, blk = x_ref.shape[1], x_ref.shape[2]

    def place(t, c):
        return xall_ref.at[
            pl.ds(pl.multiple_of(c * c_all, 8), c_all), pl.ds(pl.multiple_of(t * blk, 128), blk)
        ]

    own = (win_ref, whid_ref)
    full = (winall_ref, whidall_ref)
    depth = (win_ref.shape[1], whid_ref.shape[1])
    locals_ = [pltpu.make_async_copy(x_ref.at[pos], place(s, me), local_sem.at[0])]
    for a in range(2):
        locals_.append(
            pltpu.make_async_copy(
                own[a], full[a].at[:, pl.ds(pl.multiple_of(me * depth[a], 8), depth[a])], local_sem.at[1 + a]
            )
        )
    order = []
    for k in range(1, n // 2 + 1):
        order.append(k)
        if n - k != k:
            order.append(n - k)
    started = []

    def start(copy):
        copy.start()
        started.append(copy)

    for d in order:
        c = others[d - 1][1]
        start(remote(x_ref.at[lax.rem(pos + d, n)], place(s, me), a2a_send.at[d], a2a_recv.at[n - d], (s, c)))
    units = weight_units(*depth)
    for direction in range(2):
        target = (s, (right, left)[direction])
        for u, (a, g, r0, rows) in enumerate(units[direction]):
            start(
                remote(
                    own[a].at[g, pl.ds(r0, rows)],
                    full[a].at[g, pl.ds(pl.multiple_of(me * depth[a] + r0, 8), rows)],
                    ring_send.at[direction, 0, u], ring_recv.at[direction, 0, u], target,
                )
            )
    for copy in locals_:
        copy.start()

    def forward(d, c):
        block = place(s, c)
        for i, t in enumerate(xpeers):
            start(remote(block, block, x_send.at[i, d], x_recv.at[i, d], (t, me)))
        start(remote(block, block, sib_send.at[0, d], sib_recv.at[0, d], (sib, me)))

    locals_[0].wait()
    forward(0, me)
    for d in order:
        c = others[d - 1][1]
        remote(place(s, c), place(s, c), a2a_send.at[0], a2a_recv.at[d], (s, c)).wait_recv()
        forward(d, c)

    def from_x(d):
        c = ring_chan(lax.rem(pos + d, n), n)
        n_x = len(xpeers) + 1
        for i in range(n_x - 1):
            block = place(xpeers[n_x - 2 - i], c)
            remote(block, block, x_send.at[i, d], x_recv.at[i, d], (sib, me)).wait_recv()
            start(remote(block, block, sib_send.at[1 + i, d], sib_recv.at[1 + i, d], (sib, me)))

    pending = [0] + order
    for step in range(n - 1):
        for u in range(max(len(units[0]), len(units[1]))):
            for direction in range(2):
                if u >= len(units[direction]):
                    continue
                a, g, r0, rows = units[direction][u]
                origin = lax.rem(pos + (n - 1 - step if direction == 0 else step + 1), n)
                oc = ring_chan(origin, n)
                block = full[a].at[g, pl.ds(pl.multiple_of(oc * depth[a] + r0, 8), rows)]
                target = (s, (right, left)[direction])
                remote(block, block, ring_send.at[direction, step, u], ring_recv.at[direction, step, u], target).wait_recv()
                if step < n - 2:
                    start(
                        remote(
                            block, block, ring_send.at[direction, step + 1, u],
                            ring_recv.at[direction, step + 1, u], target,
                        )
                    )
        if step >= 1 and pending:
            for _ in range(2):
                if pending:
                    from_x(pending.pop(0))
    for d in pending:
        from_x(d)
    for d in [0] + order:
        c = ring_chan(lax.rem(pos + d, n), n)
        sib_s = sib
        block = place(sib_s, c)
        remote(block, block, sib_send.at[0, d], sib_recv.at[0, d], (sib, me)).wait_recv()
        n_x = len(xpeers) + 1
        for i in range(n_x - 1):
            src_s = xpeers[n_x - 2 - i]
            core = lax.rem(s, CORES)
            block = place(src_s + 1 - 2 * core, c)
            remote(block, block, sib_send.at[1 + i, d], sib_recv.at[1 + i, d], (sib, me)).wait_recv()
    for copy in started:
        copy.wait_send()
    for copy in locals_[1:]:
        copy.wait()


def share_kernel(
    n_space, n, v_ref, e_ref, all_ref, halo_ref,
    near_send, near_recv, x_send, x_recv, sib_send, sib_recv, local_sem,
):
    s, xpeers, sib = lines(n_space)
    me = lax.axis_index("chan")
    pos = ring_pos(me, n)
    right, left = ring_chan(lax.rem(pos + 1, n), n), ring_chan(lax.rem(pos + n - 1, n), n)
    barrier([(s, left), (s, right)] + [(t, me) for t in xpeers] + [(sib, me)])
    outs, edge = e_ref.shape

    def place(ref, t):
        return ref.at[pl.ds(pl.multiple_of(t * outs, 8), outs)]

    from_left = halo_ref.at[pl.ds(pl.multiple_of(s * outs, 8), outs), pl.ds(0, edge)]
    from_right = halo_ref.at[pl.ds(pl.multiple_of(s * outs, 8), outs), pl.ds(edge, edge)]
    started = []

    def start(copy):
        copy.start()
        started.append(copy)

    start(remote(e_ref, from_right, near_send.at[0], near_recv.at[0], (s, left)))
    start(remote(e_ref, from_left, near_send.at[1], near_recv.at[1], (s, right)))
    for i, t in enumerate(xpeers):
        start(remote(v_ref, place(all_ref, s), x_send.at[i, 0], x_recv.at[i, 0], (t, me)))
    start(remote(v_ref, place(all_ref, s), sib_send.at[0, 0], sib_recv.at[0, 0], (sib, me)))
    local = pltpu.make_async_copy(v_ref, place(all_ref, s), local_sem)
    local.start()
    remote(e_ref, from_right, near_send.at[0], near_recv.at[0], (s, left)).wait_recv()
    remote(e_ref, from_left, near_send.at[1], near_recv.at[1], (s, right)).wait_recv()
    h = place(halo_ref, s)
    for i, t in enumerate(xpeers):
        start(remote(h, h, x_send.at[i, 1], x_recv.at[i, 1], (t, me)))
    start(remote(h, h, sib_send.at[0, 1], sib_recv.at[0, 1], (sib, me)))
    n_x = len(xpeers) + 1
    core = lax.rem(s, CORES)
    for which, ref in ((1, halo_ref), (0, all_ref)):
        for i in range(n_x - 1):
            block = place(ref, xpeers[n_x - 2 - i])
            remote(block, block, x_send.at[i, which], x_recv.at[i, which], (sib, me)).wait_recv()
            start(remote(block, block, sib_send.at[1 + i, which], sib_recv.at[1 + i, which], (sib, me)))
    for which, ref in ((1, halo_ref), (0, all_ref)):
        block = place(ref, sib)
        remote(block, block, sib_send.at[0, which], sib_recv.at[0, which], (sib, me)).wait_recv()
        for i in range(n_x - 1):
            block = place(ref, xpeers[n_x - 2 - i] + 1 - 2 * core)
            remote(block, block, sib_send.at[1 + i, which], sib_recv.at[1 + i, which], (sib, me)).wait_recv()
    for copy in started:
        copy.wait_send()
    local.wait()


def return_kernel(n_space, n, v_ref, out_ref, send, recv, local_sem):
    s = lax.axis_index("space")
    me = lax.axis_index("chan")
    pos = ring_pos(me, n)
    share = n // n_space
    owner = me // share
    k_hid, blk = out_ref.shape[1], out_ref.shape[2]

    def piece(k):
        return v_ref.at[pl.ds(k % share * k_hid, k_hid), pl.ds(k // share * blk, blk)]

    sem = pltpu.get_barrier_semaphore()
    here = owner == s

    def each_source(act):
        for p in range(n):
            c = ring_chan(jnp.int32(p), n)
            act(p, c, jnp.logical_and(here, c == me))

    def each_target(act):
        for k in range(n_space * share):
            t, c = k // share, share * s + k % share
            act(k, t, c, jnp.logical_and(t == s, c == me))

    def hello(p, c, self_):
        @pl.when(jnp.logical_not(self_))
        def _():
            pl.semaphore_signal(sem, inc=1, device_id=(owner, c), device_id_type=MESH)

    each_source(hello)
    pl.semaphore_wait(sem, jnp.where(here, n_space * share - 1, n_space * share))

    def send_one(k, t, c, self_):
        @pl.when(jnp.logical_not(self_))
        def _():
            remote(piece(k), out_ref.at[pos], send.at[k], recv.at[pos], (t, c)).start()

        @pl.when(self_)
        def _():
            pltpu.make_async_copy(piece(k), out_ref.at[pos], local_sem).start()

    each_target(send_one)

    def wait_one(p, c, self_):
        @pl.when(jnp.logical_not(self_))
        def _():
            remote(piece(0), out_ref.at[p], send.at[0], recv.at[p], (owner, c)).wait_recv()

    each_source(wait_one)

    def sent_one(k, t, c, self_):
        @pl.when(jnp.logical_not(self_))
        def _():
            remote(piece(k), out_ref.at[pos], send.at[k], recv.at[pos], (t, c)).wait_send()

        @pl.when(self_)
        def _():
            pltpu.make_async_copy(piece(k), out_ref.at[pos], local_sem).wait()

    each_target(sent_one)


ANY = pl.BlockSpec(memory_space=pl.ANY)


def dma(*shape):
    return pltpu.SemaphoreType.DMA(shape)


def lanes_in(shape, first, last, stride):
    col = lax.rem(lax.broadcasted_iota(jnp.int32, shape, 1), stride)
    return jnp.logical_and(col >= first, col <= last)


def tap_products(weight, x_ref, y_ref):
    width = 512

    @pl.loop(0, x_ref.shape[1] // width)
    def _(j):
        at = pl.ds(pl.multiple_of(j * width, width), width)
        y_ref[:, at] = jnp.dot(weight[...], x_ref[:, at], preferred_element_type=jnp.float32)


def shift_add(y_ref, stride, store):
    outs, length = y_ref.shape[0] // 9, y_ref.shape[1]

    @pl.loop(0, outs // 8)
    def _(i):
        lane = lax.broadcasted_iota(jnp.int32, (8, length), 1)
        total = None
        for row_off in (-1, 0, 1):
            part = None
            for col_off in (-1, 0, 1):
                tap = 3 * (row_off + 1) + col_off + 1
                value = y_ref[pl.ds(pl.multiple_of(tap * outs + i * 8, 8), 8), :]
                shift = (-(row_off * stride + col_off)) % length
                if shift:
                    value = pltpu.roll(value, shift, 1)
                part = value if part is None else part + value
            if row_off == -1:
                part = jnp.where(lane < stride, 0.0, part)
            if row_off == 1:
                part = jnp.where(lane >= length - stride, 0.0, part)
            total = part if total is None else total + part
        store(pl.ds(pl.multiple_of(i * 8, 8), 8), i * 8, total)


def terms_kernel(stride, x_ref, w_ref, bias_ref, terms_ref, y_ref):
    outs = y_ref.shape[0] // 9

    @pl.loop(0, 3)
    def _(g):
        tap_products(w_ref.at[g], x_ref, y_ref)

        def store(rows, first, total):
            at = pl.ds(pl.multiple_of(g * outs + first, 8), 8)
            terms_ref[at, :] = total + bias_ref[at, :]

        shift_add(y_ref, stride, store)


def merge(x_ref, halo_ref, put_ref, full_ref):
    width = 512

    @pl.loop(0, x_ref.shape[1] // width)
    def _(j):
        at = pl.ds(pl.multiple_of(j * width, width), width)
        edges = jnp.dot(halo_ref[...], put_ref[:, at], preferred_element_type=jnp.float32)
        full_ref[:, at] = (x_ref[:, at].astype(jnp.float32) + edges).astype(jnp.bfloat16)


def finish(stride, cols, wide_ref, take_ref, value_ref, edge_ref):
    value = wide_ref[...]
    value = jnp.where(lanes_in(value.shape, 1, cols, stride), value, 0.0).astype(jnp.bfloat16)
    value_ref[...] = value
    edge_ref[...] = jnp.dot(value, take_ref[...], preferred_element_type=jnp.float32).astype(jnp.bfloat16)


def gates_kernel(
    stride, cols, merged, x_ref, halo_ref, own_ref, w_ref, terms_ref, put_ref, take_ref,
    update_ref, gated_ref, edge_ref, y_ref, wide_ref, full_ref,
):
    outs = own_ref.shape[0]
    if not merged:
        merge(x_ref, halo_ref, put_ref, full_ref)
        x_ref = full_ref
    wide_ref[...] = own_ref[...].astype(jnp.float32)

    def store_update(rows, first, total):
        update_ref[rows, :] = jax.nn.sigmoid(total + terms_ref[rows, :])

    def store_gated(rows, first, total):
        at = pl.ds(pl.multiple_of(outs + first, 8), 8)
        wide_ref[rows, :] = jax.nn.sigmoid(total + terms_ref[at, :]) * wide_ref[rows, :]

    tap_products(w_ref.at[0], x_ref, y_ref)
    shift_add(y_ref, stride, store_update)
    tap_products(w_ref.at[1], x_ref, y_ref)
    shift_add(y_ref, stride, store_gated)
    finish(stride, cols, wide_ref, take_ref, gated_ref, edge_ref)


def candidate_kernel(
    stride, cols, x_ref, halo_ref, own_ref, w_ref, terms_ref, update_ref, put_ref, take_ref,
    state_ref, edge_ref, y_ref, wide_ref, full_ref,
):
    outs = own_ref.shape[0]
    merge(x_ref, halo_ref, put_ref, full_ref)
    wide_ref[...] = own_ref[...].astype(jnp.float32)

    def store(rows, first, total):
        at = pl.ds(pl.multiple_of(2 * outs + first, 8), 8)
        candidate = jnp.tanh(total + terms_ref[at, :])
        update = update_ref[rows, :]
        wide_ref[rows, :] = (1.0 - update) * wide_ref[rows, :] + update * candidate

    tap_products(w_ref.at[2], full_ref, y_ref)
    shift_add(y_ref, stride, store)
    finish(stride, cols, wide_ref, take_ref, state_ref, edge_ref)


def compute(body, shapes, scratch, name, *operands):
    vmem = pl.BlockSpec(memory_space=pltpu.VMEM)
    return pl.pallas_call(
        body,
        out_shape=shapes,
        in_specs=[vmem] * len(operands),
        out_specs=jax.tree.map(lambda _: vmem, shapes),
        scratch_shapes=scratch,
        compiler_params=pltpu.CompilerParams(vmem_limit_bytes=60 * 1024 * 1024),
        name=name,
    )(*operands)


def per_device(inputs, initial_state, input_weight, hidden_weight, gate_bias):
    n_space, n = lax.axis_size("space"), lax.axis_size("chan")
    s, me = lax.axis_index("space"), lax.axis_index("chan")
    pos = ring_pos(me, n)
    k_in, k_hid = inputs.shape[0], initial_state.shape[0]
    band, grid = inputs.shape[1], inputs.shape[2]
    cols = grid // n
    rows = band * n_space
    hidden = k_hid * n
    outs = hidden // n_space
    stride = (cols + 2 + 7) // 8 * 8
    blk = band * stride
    length = rows * stride
    c_all = k_in + k_hid
    n_x = n_space // CORES

    both = jnp.concatenate([inputs, initial_state], 0)
    both = jnp.pad(both, ((0, 0), (0, 0), (1, stride - cols - 1)))
    blocks = jnp.stack([both[:, :, p * cols : p * cols + stride] for p in range(n)])
    blocks = blocks.reshape(n, c_all, blk)

    def own_part(weight):
        part = lax.dynamic_slice_in_dim(weight, s * outs, outs, 3)
        return part.transpose(0, 2, 1, 3).reshape(3, weight.shape[2], 9 * outs)

    xall, win, whid = pl.pallas_call(
        functools.partial(spread_kernel, n_space, n),
        out_shape=(
            jax.ShapeDtypeStruct((n * c_all, length), jnp.bfloat16),
            jax.ShapeDtypeStruct((3, k_in * n, 9 * outs), jnp.bfloat16),
            jax.ShapeDtypeStruct((3, k_hid * n, 9 * outs), jnp.bfloat16),
        ),
        in_specs=[ANY] * 3,
        out_specs=(ANY,) * 3,
        scratch_shapes=[
            dma(n), dma(n), dma(n_x - 1, n), dma(n_x - 1, n), dma(n_x, n), dma(n_x, n),
            dma(2, n - 1, 4), dma(2, n - 1, 4), dma(3),
        ],
        compiler_params=pltpu.CompilerParams(collective_id=0, has_side_effects=True),
        name="spread",
    )(blocks, own_part(input_weight), own_part(hidden_weight))

    split = xall.reshape(n, c_all, length)
    x_in = split[:, :k_in].reshape(n * k_in, length)
    state_full = split[:, k_in:].reshape(hidden, length)
    w_in, w_hid = win.swapaxes(1, 2), whid.swapaxes(1, 2)
    bias = lax.dynamic_slice_in_dim(gate_bias, s * outs, outs, 1).reshape(3 * outs, 1)

    h, p = jnp.arange(4 * rows)[:, None], jnp.arange(length)[None, :]
    put = jnp.logical_or(
        (h >= rows) & (h < 2 * rows) & (p == (h - rows) * stride) & (pos > 0),
        (h >= 2 * rows) & (h < 3 * rows) & (p == (h - 2 * rows) * stride + cols + 1) & (pos < n - 1),
    ).astype(jnp.bfloat16)
    q, e = jnp.arange(length)[:, None], jnp.arange(2 * rows)[None, :]
    take = (q == jnp.where(e < rows, e * stride + 1, (e - rows) * stride + cols)).astype(jnp.bfloat16)

    f32 = jax.ShapeDtypeStruct((outs, length), jnp.float32)
    b16 = jax.ShapeDtypeStruct((outs, length), jnp.bfloat16)
    edge = jax.ShapeDtypeStruct((outs, 2 * rows), jnp.bfloat16)
    y = pltpu.VMEM((9 * outs, length), jnp.float32)
    scratch = [y, pltpu.VMEM((outs, length), jnp.float32), pltpu.VMEM((hidden, length), jnp.bfloat16)]

    terms = compute(
        functools.partial(terms_kernel, stride),
        jax.ShapeDtypeStruct((3 * outs, length), jnp.float32), [y], "terms", x_in, w_in, bias,
    )

    def share(value, edges):
        return pl.pallas_call(
            functools.partial(share_kernel, n_space, n),
            out_shape=(
                jax.ShapeDtypeStruct((hidden, length), jnp.bfloat16),
                jax.ShapeDtypeStruct((hidden, 4 * rows), jnp.bfloat16),
            ),
            in_specs=[ANY] * 2,
            out_specs=(ANY,) * 2,
            scratch_shapes=[
                dma(2), dma(2), dma(n_x - 1, 2), dma(n_x - 1, 2), dma(n_x, 2), dma(n_x, 2),
                pltpu.SemaphoreType.DMA,
            ],
            compiler_params=pltpu.CompilerParams(collective_id=1, has_side_effects=True),
            name="share",
        )(value, edges)

    halo = jnp.zeros((hidden, 4 * rows), jnp.bfloat16)
    current = lax.dynamic_slice_in_dim(state_full, s * outs, outs, 0)
    for repeat in range(STEPS):
        if repeat > 0:
            state_full, halo = share(current, edges)
        update, gated, edges = compute(
            functools.partial(gates_kernel, stride, cols, repeat == 0), (f32, b16, edge), scratch, "gates",
            state_full, halo, current, w_hid, terms, put, take,
        )
        gated_all, gated_halo = share(gated, edges)
        current, edges = compute(
            functools.partial(candidate_kernel, stride, cols), (b16, edge), scratch, "candidate",
            gated_all, gated_halo, current, w_hid, terms, update, put, take,
        )

    back = pl.pallas_call(
        functools.partial(return_kernel, n_space, n),
        out_shape=jax.ShapeDtypeStruct((n, k_hid, blk), jnp.bfloat16),
        in_specs=[ANY],
        out_specs=ANY,
        scratch_shapes=[dma(n), dma(n), pltpu.SemaphoreType.DMA],
        compiler_params=pltpu.CompilerParams(collective_id=2, has_side_effects=True),
        name="give_back",
    )(current)
    back = back.reshape(n, k_hid, band, stride)[..., 1 : cols + 1]
    return back.transpose(1, 2, 0, 3).reshape(k_hid, band, grid)


def solution(mesh):
    placed = (
        P("chan", "space", None),
        P("chan", "space", None),
        P(None, None, "chan", None),
        P(None, None, "chan", None),
        P(),
    )
    return jax.shard_map(
        per_device, mesh=mesh, in_specs=placed, out_specs=P("chan", "space", None), check_vma=False
    )
```
